256 devices in a mesh: outer: 8 (over z), inner: 32 (over y, x, core).
Axes of the slice: x: 4, y: 4, z: 8, core: 2. Of those that a mesh axis runs over, the one named last changes fastest.
Arguments:
- context: bfloat16 [32768, 4096], P(('outer', 'inner')), may hold values from -5 to 5
- query_acts: bfloat16 [64, 4096], replicated, may hold values from -5 to 5
- norm_gain: float32 [4096], replicated, may hold values from 0.25 to 1.75
- w_query: bfloat16 [4096, 2048], P('inner'), may hold values from -0.078125 to 0.078125
- w_key: bfloat16 [4096, 512], P('inner'), may hold values from -0.453125 to 0.453125
- value_weight: bfloat16 [4096, 512], P('inner'), may hold values from -0.09375 to 0.09375
- lengths: int32 [256], replicated, may hold values from 64 to 128, as said below
Outputs:
- block_out: bfloat16 [32768, 2048], P(('outer', 'inner'))
- query_out: bfloat16 [64, 2048], replicated
The draws below stay inside these ranges and needn't reach their ends.
Inputs may be any that keep to these rules, and one draw needn't show every extreme that they name: `lengths`: valid tokens of a block are its first ones; the rest of it is padding.
All inputs are finite; a program needn't handle non-finite values.
Results may differ from the reference program's by a relative error of at most 0.004.
The reference program's roundings to bfloat16 on the way count: a program that leaves them out, or rounds other values in their place, can miss the bound.
Values may be sent and summed in bfloat16 or wider, within the bound.
No kernel may reach another device: no remote copies, remote signals or barrier semaphores. Data moves between devices by JAX's collectives and lax.ppermute only.
A program may use at most 320 MiB of HBM per device.

```python
import jax
import jax.numpy as jnp
from jax import lax

MODEL_WIDTH = 4096
QUERY_HEADS = 16
KEY_VALUE_HEADS = 4
HEAD_SIZE = 128
BLK = 128
QTOK = 64
TOKENS = 32768


def coarse_rows(stream, extent):
    return jnp.clip(jax.random.normal(stream, extent, jnp.float32), -5.0, 5.0)


def query_probs(key):
    return coarse_rows(jax.random.fold_in(key, 17), (MODEL_WIDTH, QUERY_HEADS * HEAD_SIZE)) * MODEL_WIDTH ** (-0.5)


def draw_context(key, part):
    drawn = coarse_rows(jax.random.fold_in(key, 11), (TOKENS, MODEL_WIDTH))
    return drawn.astype(jnp.bfloat16)


def draw_query_acts(key, part):
    drawn = coarse_rows(jax.random.fold_in(key, 13), (QTOK, MODEL_WIDTH))
    return drawn.astype(jnp.bfloat16)


def draw_w_query(key, part):
    return query_probs(key).astype(jnp.bfloat16)


def draw_w_key(key, part):
    small_noise = coarse_rows(jax.random.fold_in(key, 23), (MODEL_WIDTH, KEY_VALUE_HEADS * HEAD_SIZE)) * MODEL_WIDTH ** (-0.5)
    return small_noise.astype(jnp.bfloat16)


def draw_lengths(key, part):
    blocks = TOKENS // BLK
    drawn = jax.random.randint(jax.random.fold_in(key, 41), (blocks,), BLK // 2, BLK + 1, dtype=jnp.int32)
    longest = jax.random.randint(jax.random.fold_in(key, 42), (), 0, blocks, dtype=jnp.int32)
    shortest = (longest + 1 + jax.random.randint(jax.random.fold_in(key, 43), (), 0, blocks - 1, dtype=jnp.int32)) % blocks
    places = jnp.arange(blocks, dtype=jnp.int32)
    drawn = jnp.where(places == longest, BLK, drawn)
    return jnp.where(places == shortest, BLK // 2, drawn).astype(jnp.int32)


def block_scale(stream_key, dims, shards, least, high):
    def one(dim, shards_of):
        draws = jax.random.uniform(jax.random.fold_in(jax.random.fold_in(stream_key, 6), dim), (shards_of,), jnp.float32, least / len(shards), high / len(shards))
        return jnp.repeat(jnp.exp(draws), dims[dim] // shards_of).reshape((-1,) + (1,) * (len(dims) - dim - 1))

    factor_of = one(*shards[0])
    for cut in shards[1:]:
        factor_of = factor_of * one(*cut)
    return factor_of


def centred(key, shape, deviation, limit, cuts=(), kind=jnp.bfloat16):
    factor_of = block_scale(key, shape, cuts, -0.22, 0.18) if cuts else 1.0
    array = jax.random.normal(key, shape, jnp.float32) * deviation * factor_of
    return jnp.minimum(jnp.maximum(array, -limit), limit).astype(kind)


def setup_inputs(seed: int = 0) -> dict:
    key_list = jax.random.split(jax.random.key(seed), 8)
    return {
        "context": draw_context(jax.random.fold_in(key_list[7], 71), 0),
        "query_acts": draw_query_acts(jax.random.fold_in(key_list[7], 71), 0),
        "norm_gain": jnp.clip(1.0 + 0.15 * jax.random.normal(key_list[2], (MODEL_WIDTH,), jnp.float32), 0.25, 1.75),
        "w_query": draw_w_query(jax.random.fold_in(key_list[7], 71), 0),
        "w_key": draw_w_key(jax.random.fold_in(key_list[7], 71), 0),
        "value_weight": centred(key_list[5], (MODEL_WIDTH, KEY_VALUE_HEADS * HEAD_SIZE), MODEL_WIDTH ** -0.5, 0.09375, ((0, 32),)),
        "lengths": draw_lengths(jax.random.fold_in(key_list[7], 71), 0),
    }


epsilon = 1e-05

def normalize(matrix, norm_gain):
    widened = matrix.astype(jnp.float32)
    factor = lax.rsqrt(lax.optimization_barrier(jnp.mean(widened * widened, axis=-1, keepdims=True)) + epsilon)
    return (widened * factor * norm_gain).astype(jnp.bfloat16)

def project(normed, weight):
    return jnp.dot(normed, weight, preferred_element_type=jnp.float32).astype(jnp.bfloat16)

def widen_rounded(value_matrix):
    return lax.optimization_barrier(value_matrix.astype(jnp.bfloat16)).astype(jnp.float32)

def attend_part(query_rows, key_row_block, value_matrix, allowed):
    count_of_rows = query_rows.shape[0]
    head_groups = query_rows.reshape(count_of_rows, KEY_VALUE_HEADS, QUERY_HEADS // KEY_VALUE_HEADS, HEAD_SIZE).astype(jnp.float32)
    per_head_keys = key_row_block.reshape(key_row_block.shape[0], KEY_VALUE_HEADS, HEAD_SIZE).astype(jnp.float32)
    per_head_values = value_matrix.reshape(value_matrix.shape[0], KEY_VALUE_HEADS, HEAD_SIZE).astype(jnp.float32)
    scores = jnp.einsum('rhgd,khd->hgrk', head_groups, per_head_keys) * HEAD_SIZE ** (-0.5)
    scores = jnp.where(allowed, scores, -jnp.inf)
    maxima = lax.optimization_barrier(jnp.max(scores, axis=-1))
    weights = jnp.exp(scores - maxima[..., None])
    sum_exp = lax.optimization_barrier(jnp.sum(weights, axis=-1))
    numerator = jnp.einsum('hgrk,khd->rhgd', widen_rounded(weights), per_head_values)
    return (maxima.reshape(QUERY_HEADS, count_of_rows), sum_exp.reshape(QUERY_HEADS, count_of_rows), numerator.reshape(count_of_rows, QUERY_HEADS * HEAD_SIZE))

def spread(factor):
    return jnp.repeat(factor.T, HEAD_SIZE, axis=1)

def combine(former, latter):
    maxima = jnp.maximum(former[0], latter[0])
    scale_one = jnp.exp(former[0] - maxima)
    scale_two = jnp.exp(latter[0] - maxima)
    return (maxima, former[1] * scale_one + latter[1] * scale_two, former[2] * spread(scale_one) + latter[2] * spread(scale_two))

def finish(pieces):
    return (pieces[2] / spread(pieces[1])).astype(jnp.bfloat16)

def reference(context, query_acts, norm_gain, w_query, w_key, value_weight, lengths):
    block_count = lengths.shape[0]
    anchor_normed = normalize(context[:BLK], norm_gain)
    anchor_keys = project(anchor_normed, w_key)
    anchor_values = project(anchor_normed, value_weight)
    anchor_length = lengths[0]
    query_normed = normalize(query_acts, norm_gain)
    query_q = project(query_normed, w_query)
    query_k = project(query_normed, w_key)
    query_v = project(query_normed, value_weight)
    places = jnp.arange(BLK, dtype=jnp.int32)
    causal = places[:, None] >= places[None, :]

    def one_block(running, inputs):
        matrix, length, block_index = inputs
        normed = normalize(matrix, norm_gain)
        block_q = project(normed, w_query)
        block_k = project(normed, w_key)
        block_v = project(normed, value_weight)
        own_allowed = causal & (places[None, :] < length)
        anchor_allowed = jnp.broadcast_to((places[None, :] < anchor_length) & (block_index > 0), (BLK, BLK))
        allowed = jnp.concatenate([anchor_allowed, own_allowed], axis=1)
        key_row_block = jnp.concatenate([anchor_keys, block_k], axis=0)
        value_rows = jnp.concatenate([anchor_values, block_v], axis=0)
        outputs = finish(attend_part(block_q, key_row_block, value_rows, allowed))
        reached = jnp.broadcast_to(places[None, :] < length, (QTOK, BLK))
        running = combine(running, attend_part(query_q, block_k, block_v, reached))
        return (running, outputs)
    initial = (jnp.full((QUERY_HEADS, QTOK), -jnp.inf, jnp.float32), jnp.zeros((QUERY_HEADS, QTOK), jnp.float32), jnp.zeros((QTOK, QUERY_HEADS * HEAD_SIZE), jnp.float32))
    running, outputs = lax.scan(one_block, initial, (context.reshape(block_count, BLK, MODEL_WIDTH), lengths, jnp.arange(block_count, dtype=jnp.int32)))
    query_places = jnp.arange(QTOK, dtype=jnp.int32)
    self_part = attend_part(query_q, query_k, query_v, query_places[:, None] >= query_places[None, :])
    query_out = finish(combine(running, self_part))
    return (outputs.reshape(block_count * BLK, QUERY_HEADS * HEAD_SIZE), query_out)
```

```python
import functools

import jax
import jax.numpy as jnp
from jax import lax
from jax.experimental import pallas as pl
from jax.experimental.pallas import tpu as pltpu
from jax.sharding import Mesh
from jax.sharding import PartitionSpec as P

HEAD_SIZE = 128
GROUP_HEADS = 4
BLK = 128
QTOK = 64
PAIRS = GROUP_HEADS * QTOK
CHIPS = 16
SHARE = PAIRS // CHIPS
ANCHOR_SHARE = BLK // CHIPS
SCALE = HEAD_SIZE ** (-0.5)
EPSILON = 1e-05
AXES = ("zg", "zi", "y", "x", "core")
PLANE = ("y", "x")
YXC = ("y", "x", "core")
OFFSETS = (0, -1, 1, 2)
bf16 = jnp.bfloat16
f32 = jnp.float32
VMEM = pl.BlockSpec(memory_space=pltpu.VMEM)
SMEM = pl.BlockSpec(memory_space=pltpu.SMEM)
SWAP = [(0, 1), (1, 0)]


def device_index(y, x, core):
    return (y * 4 + x) * 2 + core


def torus_pairs(step, first):
    pairs = []
    for y in range(4):
        for x in range(4):
            for core in range(2):
                along_x = (core == 0) == first
                to = (y, (x + step) % 4) if along_x else ((y + step) % 4, x)
                pairs.append((device_index(y, x, core), device_index(*to, core)))
    return pairs


def ring(piece, first):
    half = piece.shape[0] // 2
    send = lambda rows, step: lax.ppermute(rows, YXC, torus_pairs(step, first))
    before, after = send(piece, 1), send(piece, -1)
    return before, after, send(before[:half], 1), send(after[half:], -1)


def prepare_kernel(place, own, core_mate, z_mate, zc_mate, query, gain, *outs):
    y, x, core = place[0], place[1], place[2]
    step = 64
    for number, ref in enumerate((own, core_mate, z_mate, zc_mate, query)):
        for start in range(0, ref.shape[0], step):
            widened = ref[start : start + step, :].astype(f32)
            factor = lax.rsqrt(jnp.mean(widened * widened, axis=-1, keepdims=True) + EPSILON)
            rows = slice(number * BLK + start, number * BLK + start + step)
            for b in range(4):
                for a in range(4):
                    dx = jnp.where(core == 0, OFFSETS[a], OFFSETS[b])
                    dy = jnp.where(core == 0, OFFSETS[b], OFFSETS[a])
                    chip = ((y + dy) & 3) * 4 + ((x + dx) & 3)
                    cols = pl.ds(pl.multiple_of(chip * 256, 256), 256)
                    part = ref[start : start + step, cols].astype(f32) * factor * gain[:, cols]
                    outs[b][rows, a * 256 : (a + 1) * 256] = part.astype(bf16)


def query_kernel(place, lengths, proj, packed, anchor):
    position, origin = place[3], place[4]
    q = jnp.concatenate(
        [proj[4 * BLK :, HEAD_SIZE * g : HEAD_SIZE * (g + 1)] for g in range(GROUP_HEADS)], axis=0
    )
    k = proj[:, 512:640]
    v = proj[:, 640:768]
    scores = lax.dot_general(q, k, (((1,), (1,)), ((), ())), preferred_element_type=f32) * SCALE
    keys = 4 * BLK + QTOK
    col = lax.broadcasted_iota(jnp.int32, (PAIRS, keys), 1)
    row = lax.broadcasted_iota(jnp.int32, (PAIRS, keys), 0) & (QTOK - 1)
    allowed = (col >= 4 * BLK) & (col - 4 * BLK <= row) & (origin == 1)
    for j in range(4):
        length = lengths[position ^ ((j & 1) | ((j >> 1) << 5))]
        allowed = allowed | ((col >= j * BLK) & (col < j * BLK + length))
    scores = jnp.where(allowed, scores, -jnp.inf)
    peak = jnp.max(scores, axis=-1, keepdims=True)
    weights = jnp.exp(scores - peak)
    total = jnp.sum(weights, axis=-1, keepdims=True)
    numerator = jnp.dot(weights.astype(bf16), v, preferred_element_type=f32)
    lane = lax.broadcasted_iota(jnp.int32, (PAIRS, HEAD_SIZE), 1)
    stats = jnp.where(lane < 64, peak, total)
    head = place[5]
    start = pl.multiple_of(head * BLK, BLK)
    anchor_rows = proj[pl.ds(start, BLK), 512:768].astype(f32)
    for t in range(CHIPS):
        packed[t, :SHARE, :HEAD_SIZE] = numerator[t * SHARE : (t + 1) * SHARE]
        packed[t, :SHARE, HEAD_SIZE:] = stats[t * SHARE : (t + 1) * SHARE]
        packed[t, SHARE:, :] = anchor_rows[t * ANCHOR_SHARE : (t + 1) * ANCHOR_SHARE]


def merge(parts):
    peaks = [s[:, :1] for _, s in parts]
    top = functools.reduce(jnp.maximum, peaks)
    scales = [jnp.exp(p - top) for p in peaks]
    total = sum(s[:, 127:] * w for (_, s), w in zip(parts, scales))
    numerator = sum(n * w for (n, _), w in zip(parts, scales))
    return top, total, numerator


def merge_plane_kernel(parts, out):
    top, total, numerator = merge(
        [(parts[t, :SHARE, :HEAD_SIZE], parts[t, :SHARE, HEAD_SIZE:]) for t in range(CHIPS)]
    )
    lane = lax.broadcasted_iota(jnp.int32, (SHARE, HEAD_SIZE), 1)
    out[:SHARE, :HEAD_SIZE] = numerator
    out[:SHARE, HEAD_SIZE:] = jnp.where(lane < 64, top, total)
    out[SHARE:, :] = parts[0, SHARE:, :]


def merge_deep_kernel(place, own, before, after, across, out):
    refs = (own, before, after, across)
    _, total, numerator = merge([(r[:SHARE, :HEAD_SIZE], r[:SHARE, HEAD_SIZE:]) for r in refs])
    out[:SHARE, :] = numerator / total
    zg = place[6]
    anchor = own[SHARE:, :]
    for source, ref in ((1, before), (3, after), (2, across)):
        anchor = jnp.where(zg == source, ref[SHARE:, :], anchor)
    out[SHARE : SHARE + ANCHOR_SHARE, :] = anchor[:, :HEAD_SIZE]
    out[SHARE + ANCHOR_SHARE :, :] = anchor[:, HEAD_SIZE:]


def block_kernel(place, lengths, proj, shared, *outs):
    position = place[3]
    anchor_k = shared[:, SHARE : SHARE + ANCHOR_SHARE, :].reshape(BLK, HEAD_SIZE).astype(bf16)
    anchor_v = shared[:, SHARE + ANCHOR_SHARE :, :].reshape(BLK, HEAD_SIZE).astype(bf16)
    query_out = shared[:, :SHARE, :].reshape(PAIRS, HEAD_SIZE).astype(bf16)
    rows = GROUP_HEADS * BLK
    col = lax.broadcasted_iota(jnp.int32, (rows, 2 * BLK), 1)
    row = lax.broadcasted_iota(jnp.int32, (rows, 2 * BLK), 0) & (BLK - 1)
    for j in range(4):
        block = position ^ ((j & 1) | ((j >> 1) << 5))
        anchor_length = jnp.where(block > 0, lengths[0], 0)
        allowed = (col < anchor_length) | (
            (col >= BLK) & (col - BLK <= row) & (col - BLK < lengths[block])
        )
        here = slice(j * BLK, (j + 1) * BLK)
        q = jnp.concatenate(
            [proj[here, HEAD_SIZE * g : HEAD_SIZE * (g + 1)] for g in range(GROUP_HEADS)], axis=0
        )
        k = jnp.concatenate([anchor_k, proj[here, 512:640]], axis=0)
        v = jnp.concatenate([anchor_v, proj[here, 640:768]], axis=0)
        scores = lax.dot_general(q, k, (((1,), (1,)), ((), ())), preferred_element_type=f32) * SCALE
        scores = jnp.where(allowed, scores, -jnp.inf)
        peak = jnp.max(scores, axis=-1, keepdims=True)
        weights = jnp.exp(scores - peak)
        total = jnp.sum(weights, axis=-1, keepdims=True)
        numerator = jnp.dot(weights.astype(bf16), v, preferred_element_type=f32)
        result = (numerator / total).astype(bf16)
        for g in range(GROUP_HEADS):
            cols = slice(HEAD_SIZE * g, HEAD_SIZE * (g + 1))
            outs[j][:BLK, cols] = result[g * BLK : (g + 1) * BLK]
            outs[j][BLK:, cols] = query_out[g * QTOK : (g + 1) * QTOK]


def assemble_kernel(place, *refs):
    parts, block_out, query_out = refs[:4], refs[4], refs[5]
    for j in range(4):
        cols = pl.ds(pl.multiple_of((place[5] ^ j) * 512, 512), 512)
        block_out[:, cols] = parts[j][:BLK, :]
        query_out[:, cols] = parts[j][BLK:, :]


def shapes(*items):
    return tuple(jax.ShapeDtypeStruct(s, d) for s, d in items)


def call(kernel, out_shape, n_smem, n_vmem, flops=0, size=0):
    return pl.pallas_call(
        kernel,
        out_shape=out_shape,
        in_specs=[SMEM] * n_smem + [VMEM] * n_vmem,
        out_specs=jax.tree.map(lambda _: VMEM, out_shape),
        compiler_params=pltpu.CompilerParams(vmem_limit_bytes=40 << 20),
        cost_estimate=pl.CostEstimate(flops=flops, bytes_accessed=size, transcendentals=0),
    )


def per_device(context, query_acts, norm_gain, w_query, w_key, value_weight, lengths):
    zg, zi, y, x, core = (lax.axis_index(a).astype(jnp.int32) for a in AXES)
    head = zi * 2 + core
    position = ((zg * 2 + zi) * 16 + y * 4 + x) * 2 + core
    origin = ((zg == 0) & (y == 0) & (x == 0)).astype(jnp.int32)
    place = jnp.stack([y, x, core, position, origin, head, zg, zi])

    def columns(h):
        cut = lambda w, width: lax.dynamic_slice(w, (0, h * width), (w.shape[0], width))
        return jnp.concatenate([cut(w_query, 512), cut(w_key, 128), cut(value_weight, 128)], axis=1)

    mine = columns(head)
    theirs = lax.ppermute(columns(zi * 2 + 1 - core), "core", SWAP)
    flip = core == 1
    chip_rows = jnp.concatenate(
        [jnp.where(flip, theirs, mine), jnp.where(flip, mine, theirs)], axis=0
    )
    line = jnp.concatenate([chip_rows, *ring(chip_rows, True)], axis=0)
    w_before, w_after, w_top, w_bottom = ring(line, False)

    z_mate = lax.ppermute(context, "zi", SWAP)
    core_mate = lax.ppermute(context, "core", SWAP)
    zc_mate = lax.ppermute(z_mate, "core", SWAP)
    rows = 4 * BLK + QTOK
    x_own, x_before, x_after, x_across = call(
        prepare_kernel, shapes(*[((rows, 1024), bf16)] * 4), 1, 6, 1 << 24, 10 << 20
    )(place, context, core_mate, z_mate, zc_mate, query_acts, norm_gain[None])

    dot = functools.partial(jnp.dot, preferred_element_type=f32)
    total = dot(x_own, line) + dot(x_before, w_before) + dot(x_after, w_after)
    total = total + dot(x_across[:, :512], w_top) + dot(x_across[:, 512:], w_bottom)
    proj = total.astype(bf16)

    packed = call(
        lambda p, l, r, o: query_kernel(p, l, r, o, None),
        jax.ShapeDtypeStruct((CHIPS, SHARE + ANCHOR_SHARE, 256), f32), 2, 1, 1 << 27, 2 << 20,
    )(place, lengths, proj)
    gathered = lax.all_to_all(packed, PLANE, 0, 0, tiled=True)
    merged = call(
        merge_plane_kernel, jax.ShapeDtypeStruct((SHARE + ANCHOR_SHARE, 256), f32), 0, 1, 1 << 20, 1 << 19
    )(gathered)
    deep = lambda k: lax.ppermute(merged, "zg", [(i, (i + k) % 4) for i in range(4)])
    final = call(
        merge_deep_kernel,
        jax.ShapeDtypeStruct((SHARE + 2 * ANCHOR_SHARE, HEAD_SIZE), f32), 1, 4, 1 << 20, 1 << 17,
    )(place, merged, deep(1), deep(-1), deep(2)).astype(bf16)
    shared = lax.all_to_all(
        jnp.broadcast_to(final[None], (CHIPS, *final.shape)), PLANE, 0, 0, tiled=True
    )
    pieces = call(
        block_kernel, shapes(*[((BLK + QTOK, 512), bf16)] * 4), 2, 2, 1 << 29, 3 << 20
    )(place, lengths, proj, shared)
    received = (
        pieces[0],
        lax.ppermute(pieces[1], "core", SWAP),
        lax.ppermute(pieces[2], "zi", SWAP),
        lax.ppermute(pieces[3], ("zi", "core"), [(i, 3 - i) for i in range(4)]),
    )
    return call(
        assemble_kernel, shapes(((BLK, 2048), bf16), ((QTOK, 2048), bf16)), 1, 4, 0, 2 << 20
    )(place, *received)


def solution(mesh):
    grid = Mesh(mesh.devices.reshape(4, 2, 4, 4, 2), AXES)
    own_rows, width = P(AXES, None), P(YXC, None)
    return jax.shard_map(
        per_device,
        mesh=grid,
        in_specs=(own_rows, P(), P(), width, width, width, P()),
        out_specs=(own_rows, P()),
        check_vma=False,
    )
```

```python
import functools

import jax
import jax.numpy as jnp
from jax import lax
from jax.experimental import pallas as pl
from jax.experimental.pallas import tpu as pltpu
from jax.sharding import Mesh
from jax.sharding import PartitionSpec as P

HEAD_SIZE = 128
GROUP_HEADS = 4
BLK = 128
QTOK = 64
PAIRS = GROUP_HEADS * QTOK
CHIPS = 16
SHARE = PAIRS // CHIPS
ANCHOR_SHARE = BLK // CHIPS
SCALE = HEAD_SIZE ** (-0.5)
EPSILON = 1e-05
AXES = ("zg", "zi", "y", "x", "core")
PLANE = ("y", "x")
YXC = ("y", "x", "core")
OFFSETS = (0, -1, 1, 2)
bf16 = jnp.bfloat16
f32 = jnp.float32
VMEM = pl.BlockSpec(memory_space=pltpu.VMEM)
SMEM = pl.BlockSpec(memory_space=pltpu.SMEM)
SWAP = [(0, 1), (1, 0)]


def device_index(y, x, core):
    return (y * 4 + x) * 2 + core


def torus_pairs(step, first):
    pairs = []
    for y in range(4):
        for x in range(4):
            for core in range(2):
                along_x = (core == 0) == first
                to = (y, (x + step) % 4) if along_x else ((y + step) % 4, x)
                pairs.append((device_index(y, x, core), device_index(*to, core)))
    return pairs


def send(rows, step, first):
    return lax.ppermute(rows, YXC, torus_pairs(step, first))


def join(top, bottom):
    return jnp.concatenate([top, bottom], axis=0)


def gather_weights(mine, theirs):
    mate = lax.ppermute(theirs, "core", SWAP)
    own = join(mine, mate)
    before, after = send(own, 1, True), send(own, -1, True)
    across = join(send(mine, 2, True), send(mate, -2, True))
    near, far = join(own, before), join(after, across)
    near_before, far_after = send(near, 1, False), send(far, -1, False)
    far_before, near_after = send(far, 1, False), send(near, -1, False)
    near_across, far_across = send(near_before, 1, False), send(far_after, -1, False)
    return (near, far), (near_before, far_before), (near_after, far_after), (near_across, far_across)


def prepare_kernel(place, own, core_mate, z_mate, zc_mate, query, gain, *outs):
    y, x, core = place[0], place[1], place[2]
    step = 64
    for number, ref in enumerate((own, core_mate, z_mate, zc_mate, query)):
        for start in range(0, ref.shape[0], step):
            widened = ref[start : start + step, :].astype(f32)
            factor = lax.rsqrt(jnp.mean(widened * widened, axis=-1, keepdims=True) + EPSILON)
            rows = slice(number * BLK + start, number * BLK + start + step)
            for b in range(4):
                for a in range(4):
                    dx = jnp.where(core == 0, OFFSETS[a], OFFSETS[b])
                    dy = jnp.where(core == 0, OFFSETS[b], OFFSETS[a])
                    chip = ((y + dy) & 3) * 4 + ((x + dx) & 3)
                    for h in range(2):
                        source = chip * 2 + (core ^ h)
                        cols = pl.ds(pl.multiple_of(source * 128, 128), 128)
                        part = ref[start : start + step, cols].astype(f32) * factor * gain[:, cols]
                        place_in = a * 256 + h * 128
                        outs[b][rows, place_in : place_in + 128] = part.astype(bf16)


def multiply(rows, parts, cols):
    weights = jnp.concatenate([p[:, cols] for p in parts], axis=0)
    return jnp.dot(rows[...], weights, preferred_element_type=f32)


COLUMNS = [slice(n, n + 256) for n in range(0, 768, 256)]


def project_kernel(own, before, after, *refs):
    out = refs[-1]
    for cols in COLUMNS:
        total = multiply(own, refs[:2], cols) + multiply(before, refs[2:4], cols)
        out[:, cols] = total + multiply(after, refs[4:6], cols)


def query_kernel(place, lengths, across, total, near, far, proj, packed):
    for cols in COLUMNS:
        proj[:, cols] = (total[:, cols] + multiply(across, (near, far), cols)).astype(bf16)
    position, origin = place[3], place[4]
    q = jnp.concatenate(
        [proj[4 * BLK :, HEAD_SIZE * g : HEAD_SIZE * (g + 1)] for g in range(GROUP_HEADS)], axis=0
    )
    sets = []
    for j in range(5):
        keys = BLK if j < 4 else QTOK
        here = slice(j * BLK, j * BLK + keys)
        scores = lax.dot_general(
            q, proj[here, 512:640], (((1,), (1,)), ((), ())), preferred_element_type=f32
        ) * SCALE
        col = lax.broadcasted_iota(jnp.int32, (PAIRS, keys), 1)
        if j < 4:
            allowed = col < lengths[position ^ ((j & 1) | ((j >> 1) << 5))]
        else:
            allowed = col <= (lax.broadcasted_iota(jnp.int32, (PAIRS, keys), 0) & (QTOK - 1))
        scores = jnp.where(allowed, scores, -jnp.inf)
        peak = jnp.max(scores, axis=-1, keepdims=True)
        weights = jnp.exp(scores - peak)
        sum_exp = jnp.sum(weights, axis=-1, keepdims=True)
        numerator = jnp.dot(weights.astype(bf16), proj[here, 640:768], preferred_element_type=f32)
        if j == 4:
            peak = jnp.where(origin == 1, peak, -jnp.inf)
        sets.append((peak, sum_exp, numerator))
    peak = functools.reduce(jnp.maximum, [s[0] for s in sets])
    scales = [jnp.exp(s[0] - peak) for s in sets]
    total_exp = sum(s[1] * w for s, w in zip(sets, scales))
    numerator = sum(s[2] * w for s, w in zip(sets, scales))
    lane = lax.broadcasted_iota(jnp.int32, (PAIRS, HEAD_SIZE), 1)
    stats = jnp.where(lane < 64, peak, total_exp)
    start = pl.multiple_of(place[5] * BLK, BLK)
    anchor_rows = proj[pl.ds(start, BLK), 512:768].astype(f32)
    for t in range(CHIPS):
        packed[t, :SHARE, :HEAD_SIZE] = numerator[t * SHARE : (t + 1) * SHARE]
        packed[t, :SHARE, HEAD_SIZE:] = stats[t * SHARE : (t + 1) * SHARE]
        packed[t, SHARE:, :] = anchor_rows[t * ANCHOR_SHARE : (t + 1) * ANCHOR_SHARE]


def merge(parts):
    peaks = [s[:, :1] for _, s in parts]
    top = functools.reduce(jnp.maximum, peaks)
    scales = [jnp.exp(p - top) for p in peaks]
    total = sum(s[:, 127:] * w for (_, s), w in zip(parts, scales))
    numerator = sum(n * w for (n, _), w in zip(parts, scales))
    return top, total, numerator


def merge_plane_kernel(parts, out):
    top, total, numerator = merge(
        [(parts[t, :SHARE, :HEAD_SIZE], parts[t, :SHARE, HEAD_SIZE:]) for t in range(CHIPS)]
    )
    lane = lax.broadcasted_iota(jnp.int32, (SHARE, HEAD_SIZE), 1)
    out[:SHARE, :HEAD_SIZE] = numerator
    out[:SHARE, HEAD_SIZE:] = jnp.where(lane < 64, top, total)
    out[SHARE:, :] = parts[0, SHARE:, :]


def merge_deep_kernel(place, own, before, after, across, out):
    refs = (own, before, after, across)
    _, total, numerator = merge([(r[:SHARE, :HEAD_SIZE], r[:SHARE, HEAD_SIZE:]) for r in refs])
    out[:SHARE, :] = numerator / total
    zg = place[6]
    anchor = own[SHARE:, :]
    for source, ref in ((1, before), (3, after), (2, across)):
        anchor = jnp.where(zg == source, ref[SHARE:, :], anchor)
    out[SHARE : SHARE + ANCHOR_SHARE, :] = anchor[:, :HEAD_SIZE]
    out[SHARE + ANCHOR_SHARE :, :] = anchor[:, HEAD_SIZE:]


def block_kernel(place, lengths, proj, shared, *outs):
    position = place[3]
    anchor_k = shared[:, SHARE : SHARE + ANCHOR_SHARE, :].reshape(BLK, HEAD_SIZE).astype(bf16)
    anchor_v = shared[:, SHARE + ANCHOR_SHARE :, :].reshape(BLK, HEAD_SIZE).astype(bf16)
    query_out = shared[:, :SHARE, :].reshape(PAIRS, HEAD_SIZE).astype(bf16)
    rows = GROUP_HEADS * BLK
    col = lax.broadcasted_iota(jnp.int32, (rows, 2 * BLK), 1)
    row = lax.broadcasted_iota(jnp.int32, (rows, 2 * BLK), 0) & (BLK - 1)
    for j in range(4):
        block = position ^ ((j & 1) | ((j >> 1) << 5))
        anchor_length = jnp.where(block > 0, lengths[0], 0)
        allowed = (col < anchor_length) | (
            (col >= BLK) & (col - BLK <= row) & (col - BLK < lengths[block])
        )
        here = slice(j * BLK, (j + 1) * BLK)
        q = jnp.concatenate(
            [proj[here, HEAD_SIZE * g : HEAD_SIZE * (g + 1)] for g in range(GROUP_HEADS)], axis=0
        )
        k = jnp.concatenate([anchor_k, proj[here, 512:640]], axis=0)
        v = jnp.concatenate([anchor_v, proj[here, 640:768]], axis=0)
        scores = lax.dot_general(q, k, (((1,), (1,)), ((), ())), preferred_element_type=f32) * SCALE
        scores = jnp.where(allowed, scores, -jnp.inf)
        peak = jnp.max(scores, axis=-1, keepdims=True)
        weights = jnp.exp(scores - peak)
        total = jnp.sum(weights, axis=-1, keepdims=True)
        numerator = jnp.dot(weights.astype(bf16), v, preferred_element_type=f32)
        result = (numerator / total).astype(bf16)
        for g in range(GROUP_HEADS):
            cols = slice(HEAD_SIZE * g, HEAD_SIZE * (g + 1))
            outs[j][:BLK, cols] = result[g * BLK : (g + 1) * BLK]
            outs[j][BLK:, cols] = query_out[g * QTOK : (g + 1) * QTOK]


def assemble_kernel(place, *refs):
    parts, block_out, query_out = refs[:4], refs[4], refs[5]
    for j in range(4):
        cols = pl.ds(pl.multiple_of((place[5] ^ j) * 512, 512), 512)
        block_out[:, cols] = parts[j][:BLK, :]
        query_out[:, cols] = parts[j][BLK:, :]


def shapes(*items):
    return tuple(jax.ShapeDtypeStruct(s, d) for s, d in items)


def call(kernel, out_shape, n_smem, n_vmem, flops=0, size=0):
    return pl.pallas_call(
        kernel,
        out_shape=out_shape,
        in_specs=[SMEM] * n_smem + [VMEM] * n_vmem,
        out_specs=jax.tree.map(lambda _: VMEM, out_shape),
        compiler_params=pltpu.CompilerParams(vmem_limit_bytes=40 << 20),
        cost_estimate=pl.CostEstimate(flops=flops, bytes_accessed=size, transcendentals=0),
    )


def per_device(context, query_acts, norm_gain, w_query, w_key, value_weight, lengths):
    zg, zi, y, x, core = (lax.axis_index(a).astype(jnp.int32) for a in AXES)
    head = zi * 2 + core
    position = ((zg * 2 + zi) * 16 + y * 4 + x) * 2 + core
    origin = ((zg == 0) & (y == 0) & (x == 0)).astype(jnp.int32)
    place = jnp.stack([y, x, core, position, origin, head, zg, zi])

    def columns(h):
        cut = lambda w, width: lax.dynamic_slice(w, (0, h * width), (w.shape[0], width))
        return jnp.concatenate([cut(w_query, 512), cut(w_key, 128), cut(value_weight, 128)], axis=1)

    theirs = columns(zi * 2 + 1 - core)
    w_own, w_before, w_after, w_across = gather_weights(columns(head), theirs)

    z_mate = lax.ppermute(context, "zi", SWAP)
    core_mate = lax.ppermute(context, "core", SWAP)
    z_mate, _ = lax.optimization_barrier((z_mate, w_own[1]))
    zc_mate = lax.ppermute(z_mate, "core", SWAP)
    rows = 4 * BLK + QTOK
    x_own, x_before, x_after, x_across = call(
        prepare_kernel, shapes(*[((rows, 1024), bf16)] * 4), 1, 6, 1 << 24, 10 << 20
    )(place, context, core_mate, z_mate, zc_mate, query_acts, norm_gain[None])

    total = call(
        project_kernel, jax.ShapeDtypeStruct((rows, 768), f32), 0, 9, 27 << 27, 12 << 20
    )(x_own, x_before, x_after, *w_own, *w_before, *w_after)
    proj, packed = call(
        query_kernel,
        shapes(((rows, 768), bf16), ((CHIPS, SHARE + ANCHOR_SHARE, 256), f32)), 2, 4, 9 << 27, 6 << 20,
    )(place, lengths, x_across, total, *w_across)
    gathered = lax.all_to_all(packed, PLANE, 0, 0, tiled=True)
    merged = call(
        merge_plane_kernel, jax.ShapeDtypeStruct((SHARE + ANCHOR_SHARE, 256), f32), 0, 1, 1 << 20, 1 << 19
    )(gathered)
    deep = lambda k: lax.ppermute(merged, "zg", [(i, (i + k) % 4) for i in range(4)])
    final = call(
        merge_deep_kernel,
        jax.ShapeDtypeStruct((SHARE + 2 * ANCHOR_SHARE, HEAD_SIZE), f32), 1, 4, 1 << 20, 1 << 17,
    )(place, merged, deep(1), deep(-1), deep(2)).astype(bf16)
    shared = lax.all_to_all(
        jnp.broadcast_to(final[None], (CHIPS, *final.shape)), PLANE, 0, 0, tiled=True
    )
    pieces = call(
        block_kernel, shapes(*[((BLK + QTOK, 512), bf16)] * 4), 2, 2, 1 << 29, 3 << 20
    )(place, lengths, proj, shared)
    received = (
        pieces[0],
        lax.ppermute(pieces[1], "core", SWAP),
        lax.ppermute(pieces[2], "zi", SWAP),
        lax.ppermute(pieces[3], ("zi", "core"), [(i, 3 - i) for i in range(4)]),
    )
    return call(
        assemble_kernel, shapes(((BLK, 2048), bf16), ((QTOK, 2048), bf16)), 1, 4, 0, 2 << 20
    )(place, *received)


def solution(mesh):
    grid = Mesh(mesh.devices.reshape(4, 2, 4, 4, 2), AXES)
    own_rows, width = P(AXES, None), P(YXC, None)
    return jax.shard_map(
        per_device,
        mesh=grid,
        in_specs=(own_rows, P(), P(), width, width, width, P()),
        out_specs=(own_rows, P()),
        check_vma=False,
    )
```

```python
import functools

import jax
import jax.numpy as jnp
from jax import lax
from jax.experimental import pallas as pl
from jax.experimental.pallas import tpu as pltpu
from jax.sharding import Mesh
from jax.sharding import PartitionSpec as P

HEAD_SIZE = 128
GROUP_HEADS = 4
BLK = 128
QTOK = 64
PAIRS = GROUP_HEADS * QTOK
CHIPS = 16
SHARE = PAIRS // CHIPS
ANCHOR_SHARE = BLK // CHIPS
SCALE = HEAD_SIZE ** (-0.5)
EPSILON = 1e-05
AXES = ("zg", "zi", "y", "x", "core")
PLANE = ("y", "x")
YXC = ("y", "x", "core")
OFFSETS = (0, -1, 1, 2)
bf16 = jnp.bfloat16
f32 = jnp.float32
VMEM = pl.BlockSpec(memory_space=pltpu.VMEM)
SMEM = pl.BlockSpec(memory_space=pltpu.SMEM)
SWAP = [(0, 1), (1, 0)]


def device_index(y, x, core):
    return (y * 4 + x) * 2 + core


def torus_pairs(step, first):
    pairs = []
    for y in range(4):
        for x in range(4):
            for core in range(2):
                along_x = (core == 0) == first
                to = (y, (x + step) % 4) if along_x else ((y + step) % 4, x)
                pairs.append((device_index(y, x, core), device_index(*to, core)))
    return pairs


def send(rows, step, first):
    return lax.ppermute(rows, YXC, torus_pairs(step, first))


def join(top, bottom):
    return jnp.concatenate([top, bottom], axis=0)


def join_kernel(own, before, after, across, near, far):
    near[:256, :] = own[...]
    near[256:, :] = before[...]
    far[:256, :] = after[...]
    far[256:, :] = across[...]


def gather_weights(mine, theirs):
    mate = lax.ppermute(theirs, "core", SWAP)
    own = join(mine, mate)
    before, after = send(own, 1, True), send(own, -1, True)
    firsts = before, after, send(own, 2, True)
    before, after, across = lax.optimization_barrier(firsts)
    near, far = call(join_kernel, shapes(*[((512, 768), bf16)] * 2), 0, 4, 0, 3 << 20)(
        own, before, after, across
    )
    near_before, far_after = send(near, 1, False), send(far, -1, False)
    far_before, near_after = send(far, 1, False), send(near, -1, False)
    near_across, far_across = send(near_before, 1, False), send(far_after, -1, False)
    return (near, far), (near_before, far_before), (near_after, far_after), (near_across, far_across)


def prepare_kernel(place, own, core_mate, z_mate, zc_mate, query, gain, *outs):
    y, x, core = place[0], place[1], place[2]
    step = 64
    for number, ref in enumerate((own, core_mate, z_mate, zc_mate, query)):
        for start in range(0, ref.shape[0], step):
            widened = ref[start : start + step, :].astype(f32)
            factor = lax.rsqrt(jnp.mean(widened * widened, axis=-1, keepdims=True) + EPSILON)
            rows = slice(number * BLK + start, number * BLK + start + step)
            for b in range(4):
                for a in range(4):
                    dx = jnp.where(core == 0, OFFSETS[a], OFFSETS[b])
                    dy = jnp.where(core == 0, OFFSETS[b], OFFSETS[a])
                    chip = ((y + dy) & 3) * 4 + ((x + dx) & 3)
                    for h in range(2):
                        source = chip * 2 + (core ^ h)
                        cols = pl.ds(pl.multiple_of(source * 128, 128), 128)
                        part = ref[start : start + step, cols].astype(f32) * factor * gain[:, cols]
                        place_in = a * 256 + h * 128
                        outs[b][rows, place_in : place_in + 128] = part.astype(bf16)


def multiply(rows, parts, cols):
    weights = jnp.concatenate([p[:, cols] for p in parts], axis=0)
    return jnp.dot(rows[...], weights, preferred_element_type=f32)


COLUMNS = [slice(n, n + 256) for n in range(0, 768, 256)]


def project_kernel(own, before, after, *refs):
    out = refs[-1]
    for cols in COLUMNS:
        total = multiply(own, refs[:2], cols) + multiply(before, refs[2:4], cols)
        out[:, cols] = total + multiply(after, refs[4:6], cols)


def query_kernel(place, lengths, across, total, near, far, proj, packed):
    for cols in COLUMNS:
        proj[:, cols] = (total[:, cols] + multiply(across, (near, far), cols)).astype(bf16)
    position, origin = place[3], place[4]
    q = jnp.concatenate(
        [proj[4 * BLK :, HEAD_SIZE * g : HEAD_SIZE * (g + 1)] for g in range(GROUP_HEADS)], axis=0
    )
    sets = []
    for j in range(5):
        keys = BLK if j < 4 else QTOK
        here = slice(j * BLK, j * BLK + keys)
        scores = lax.dot_general(
            q, proj[here, 512:640], (((1,), (1,)), ((), ())), preferred_element_type=f32
        ) * SCALE
        col = lax.broadcasted_iota(jnp.int32, (PAIRS, keys), 1)
        if j < 4:
            allowed = col < lengths[position ^ ((j & 1) | ((j >> 1) << 5))]
        else:
            allowed = col <= (lax.broadcasted_iota(jnp.int32, (PAIRS, keys), 0) & (QTOK - 1))
        scores = jnp.where(allowed, scores, -jnp.inf)
        peak = jnp.max(scores, axis=-1, keepdims=True)
        weights = jnp.exp(scores - peak)
        sum_exp = jnp.sum(weights, axis=-1, keepdims=True)
        numerator = jnp.dot(weights.astype(bf16), proj[here, 640:768], preferred_element_type=f32)
        if j == 4:
            peak = jnp.where(origin == 1, peak, -jnp.inf)
        sets.append((peak, sum_exp, numerator))
    peak = functools.reduce(jnp.maximum, [s[0] for s in sets])
    scales = [jnp.exp(s[0] - peak) for s in sets]
    total_exp = sum(s[1] * w for s, w in zip(sets, scales))
    numerator = sum(s[2] * w for s, w in zip(sets, scales))
    lane = lax.broadcasted_iota(jnp.int32, (PAIRS, HEAD_SIZE), 1)
    stats = jnp.where(lane < 64, peak, total_exp)
    start = pl.multiple_of(place[5] * BLK, BLK)
    anchor_rows = proj[pl.ds(start, BLK), 512:768].astype(f32)
    for t in range(CHIPS):
        packed[t, :SHARE, :HEAD_SIZE] = numerator[t * SHARE : (t + 1) * SHARE]
        packed[t, :SHARE, HEAD_SIZE:] = stats[t * SHARE : (t + 1) * SHARE]
        packed[t, SHARE:, :] = anchor_rows[t * ANCHOR_SHARE : (t + 1) * ANCHOR_SHARE]


def merge(parts):
    peaks = [s[:, :1] for _, s in parts]
    top = functools.reduce(jnp.maximum, peaks)
    scales = [jnp.exp(p - top) for p in peaks]
    total = sum(s[:, 127:] * w for (_, s), w in zip(parts, scales))
    numerator = sum(n * w for (n, _), w in zip(parts, scales))
    return top, total, numerator


def merge_plane_kernel(parts, out):
    top, total, numerator = merge(
        [(parts[t, :SHARE, :HEAD_SIZE], parts[t, :SHARE, HEAD_SIZE:]) for t in range(CHIPS)]
    )
    lane = lax.broadcasted_iota(jnp.int32, (SHARE, HEAD_SIZE), 1)
    out[:SHARE, :HEAD_SIZE] = numerator
    out[:SHARE, HEAD_SIZE:] = jnp.where(lane < 64, top, total)
    out[SHARE:, :] = parts[0, SHARE:, :]


def merge_deep_kernel(place, own, before, after, across, out):
    refs = (own, before, after, across)
    _, total, numerator = merge([(r[:SHARE, :HEAD_SIZE], r[:SHARE, HEAD_SIZE:]) for r in refs])
    out[:SHARE, :] = numerator / total
    zg = place[6]
    anchor = own[SHARE:, :]
    for source, ref in ((1, before), (3, after), (2, across)):
        anchor = jnp.where(zg == source, ref[SHARE:, :], anchor)
    out[SHARE : SHARE + ANCHOR_SHARE, :] = anchor[:, :HEAD_SIZE]
    out[SHARE + ANCHOR_SHARE :, :] = anchor[:, HEAD_SIZE:]


def block_kernel(place, lengths, proj, shared, *outs):
    position = place[3]
    anchor_k = shared[:, SHARE : SHARE + ANCHOR_SHARE, :].reshape(BLK, HEAD_SIZE).astype(bf16)
    anchor_v = shared[:, SHARE + ANCHOR_SHARE :, :].reshape(BLK, HEAD_SIZE).astype(bf16)
    query_out = shared[:, :SHARE, :].reshape(PAIRS, HEAD_SIZE).astype(bf16)
    rows = GROUP_HEADS * BLK
    col = lax.broadcasted_iota(jnp.int32, (rows, 2 * BLK), 1)
    row = lax.broadcasted_iota(jnp.int32, (rows, 2 * BLK), 0) & (BLK - 1)
    for j in range(4):
        block = position ^ ((j & 1) | ((j >> 1) << 5))
        anchor_length = jnp.where(block > 0, lengths[0], 0)
        allowed = (col < anchor_length) | (
            (col >= BLK) & (col - BLK <= row) & (col - BLK < lengths[block])
        )
        here = slice(j * BLK, (j + 1) * BLK)
        q = jnp.concatenate(
            [proj[here, HEAD_SIZE * g : HEAD_SIZE * (g + 1)] for g in range(GROUP_HEADS)], axis=0
        )
        k = jnp.concatenate([anchor_k, proj[here, 512:640]], axis=0)
        v = jnp.concatenate([anchor_v, proj[here, 640:768]], axis=0)
        scores = lax.dot_general(q, k, (((1,), (1,)), ((), ())), preferred_element_type=f32) * SCALE
        scores = jnp.where(allowed, scores, -jnp.inf)
        peak = jnp.max(scores, axis=-1, keepdims=True)
        weights = jnp.exp(scores - peak)
        total = jnp.sum(weights, axis=-1, keepdims=True)
        numerator = jnp.dot(weights.astype(bf16), v, preferred_element_type=f32)
        result = (numerator / total).astype(bf16)
        for g in range(GROUP_HEADS):
            cols = slice(HEAD_SIZE * g, HEAD_SIZE * (g + 1))
            outs[j][:BLK, cols] = result[g * BLK : (g + 1) * BLK]
            outs[j][BLK:, cols] = query_out[g * QTOK : (g + 1) * QTOK]


def assemble_kernel(place, *refs):
    parts, block_out, query_out = refs[:4], refs[4], refs[5]
    for j in range(4):
        cols = pl.ds(pl.multiple_of((place[5] ^ j) * 512, 512), 512)
        block_out[:, cols] = parts[j][:BLK, :]
        query_out[:, cols] = parts[j][BLK:, :]


def shapes(*items):
    return tuple(jax.ShapeDtypeStruct(s, d) for s, d in items)


def call(kernel, out_shape, n_smem, n_vmem, flops=0, size=0):
    return pl.pallas_call(
        kernel,
        out_shape=out_shape,
        in_specs=[SMEM] * n_smem + [VMEM] * n_vmem,
        out_specs=jax.tree.map(lambda _: VMEM, out_shape),
        compiler_params=pltpu.CompilerParams(vmem_limit_bytes=40 << 20),
        cost_estimate=pl.CostEstimate(flops=flops, bytes_accessed=size, transcendentals=0),
    )


def per_device(context, query_acts, norm_gain, w_query, w_key, value_weight, lengths):
    zg, zi, y, x, core = (lax.axis_index(a).astype(jnp.int32) for a in AXES)
    head = zi * 2 + core
    position = ((zg * 2 + zi) * 16 + y * 4 + x) * 2 + core
    origin = ((zg == 0) & (y == 0) & (x == 0)).astype(jnp.int32)
    place = jnp.stack([y, x, core, position, origin, head, zg, zi])

    def columns(h):
        cut = lambda w, width: lax.dynamic_slice(w, (0, h * width), (w.shape[0], width))
        return jnp.concatenate([cut(w_query, 512), cut(w_key, 128), cut(value_weight, 128)], axis=1)

    theirs = columns(zi * 2 + 1 - core)
    w_own, w_before, w_after, w_across = gather_weights(columns(head), theirs)

    z_mate = lax.ppermute(context, "zi", SWAP)
    core_mate = lax.ppermute(context, "core", SWAP)
    z_mate, _ = lax.optimization_barrier((z_mate, w_own[1]))
    zc_mate = lax.ppermute(z_mate, "core", SWAP)
    rows = 4 * BLK + QTOK
    x_own, x_before, x_after, x_across = call(
        prepare_kernel, shapes(*[((rows, 1024), bf16)] * 4), 1, 6, 1 << 24, 10 << 20
    )(place, context, core_mate, z_mate, zc_mate, query_acts, norm_gain[None])

    total = call(
        project_kernel, jax.ShapeDtypeStruct((rows, 768), f32), 0, 9, 27 << 27, 12 << 20
    )(x_own, x_before, x_after, *w_own, *w_before, *w_after)
    proj, packed = call(
        query_kernel,
        shapes(((rows, 768), bf16), ((CHIPS, SHARE + ANCHOR_SHARE, 256), f32)), 2, 4, 9 << 27, 6 << 20,
    )(place, lengths, x_across, total, *w_across)
    gathered = lax.all_to_all(packed, PLANE, 0, 0, tiled=True)
    merged = call(
        merge_plane_kernel, jax.ShapeDtypeStruct((SHARE + ANCHOR_SHARE, 256), f32), 0, 1, 1 << 20, 1 << 19
    )(gathered)
    deep = lambda k: lax.ppermute(merged, "zg", [(i, (i + k) % 4) for i in range(4)])
    final = call(
        merge_deep_kernel,
        jax.ShapeDtypeStruct((SHARE + 2 * ANCHOR_SHARE, HEAD_SIZE), f32), 1, 4, 1 << 20, 1 << 17,
    )(place, merged, deep(1), deep(-1), deep(2)).astype(bf16)
    shared = lax.all_to_all(
        jnp.broadcast_to(final[None], (CHIPS, *final.shape)), PLANE, 0, 0, tiled=True
    )
    pieces = call(
        block_kernel, shapes(*[((BLK + QTOK, 512), bf16)] * 4), 2, 2, 1 << 29, 3 << 20
    )(place, lengths, proj, shared)
    received = (
        pieces[0],
        lax.ppermute(pieces[1], "core", SWAP),
        lax.ppermute(pieces[2], "zi", SWAP),
        lax.ppermute(pieces[3], ("zi", "core"), [(i, 3 - i) for i in range(4)]),
    )
    return call(
        assemble_kernel, shapes(((BLK, 2048), bf16), ((QTOK, 2048), bf16)), 1, 4, 0, 2 << 20
    )(place, *received)


def solution(mesh):
    grid = Mesh(mesh.devices.reshape(4, 2, 4, 4, 2), AXES)
    own_rows, width = P(AXES, None), P(YXC, None)
    return jax.shard_map(
        per_device,
        mesh=grid,
        in_specs=(own_rows, P(), P(), width, width, width, P()),
        out_specs=(own_rows, P()),
        check_vma=False,
    )
```

```python
import functools

import jax
import jax.numpy as jnp
from jax import lax
from jax.experimental import pallas as pl
from jax.experimental.pallas import tpu as pltpu
from jax.sharding import Mesh
from jax.sharding import PartitionSpec as P

HEAD_SIZE = 128
GROUP_HEADS = 4
BLK = 128
QTOK = 64
PAIRS = GROUP_HEADS * QTOK
CHIPS = 16
SHARE = PAIRS // CHIPS
ANCHOR_SHARE = BLK // CHIPS
SCALE = HEAD_SIZE ** (-0.5)
EPSILON = 1e-05
AXES = ("zg", "zi", "y", "x", "core")
PLANE = ("y", "x")
YXC = ("y", "x", "core")
OFFSETS = (0, -1, 1, 2)
bf16 = jnp.bfloat16
f32 = jnp.float32
VMEM = pl.BlockSpec(memory_space=pltpu.VMEM)
SMEM = pl.BlockSpec(memory_space=pltpu.SMEM)
SWAP = [(0, 1), (1, 0)]


def device_index(y, x, core):
    return (y * 4 + x) * 2 + core


def torus_pairs(step, first):
    pairs = []
    for y in range(4):
        for x in range(4):
            for core in range(2):
                along_x = (core == 0) == first
                to = (y, (x + step) % 4) if along_x else ((y + step) % 4, x)
                pairs.append((device_index(y, x, core), device_index(*to, core)))
    return pairs


def send(rows, step, first):
    return lax.ppermute(rows, YXC, torus_pairs(step, first))


def join(top, bottom):
    return jnp.concatenate([top, bottom], axis=0)


def join_kernel(own, before, after, across, near, far):
    near[:256, :] = own[...]
    near[256:, :] = before[...]
    far[:256, :] = after[...]
    far[256:, :] = across[...]


def gather_weights(mine, theirs):
    mate = lax.ppermute(theirs, "core", SWAP)
    own = join(mine, mate)
    before, after = send(own, 1, True), send(own, -1, True)
    firsts = before, after, send(own, 2, True)
    before, after, across = lax.optimization_barrier(firsts)
    near, far = call(join_kernel, shapes(*[((512, 768), bf16)] * 2), 0, 4, 0, 3 << 20)(
        own, before, after, across
    )
    near_before, far_after = send(near, 1, False), send(far, -1, False)
    far_before, near_after = send(far, 1, False), send(near, -1, False)
    near_across, far_across = send(near_before, 1, False), send(far_after, -1, False)
    return (near, far), (near_before, far_before), (near_after, far_after), (near_across, far_across)


def prepare_kernel(place, own, core_mate, z_mate, zc_mate, query, gain, *outs):
    y, x, core = place[0], place[1], place[2]
    step = 64
    for number, ref in enumerate((own, core_mate, z_mate, zc_mate, query)):
        for start in range(0, ref.shape[0], step):
            widened = ref[start : start + step, :].astype(f32)
            factor = lax.rsqrt(jnp.mean(widened * widened, axis=-1, keepdims=True) + EPSILON)
            rows = slice(number * BLK + start, number * BLK + start + step)
            for b in range(4):
                for a in range(4):
                    dx = jnp.where(core == 0, OFFSETS[a], OFFSETS[b])
                    dy = jnp.where(core == 0, OFFSETS[b], OFFSETS[a])
                    chip = ((y + dy) & 3) * 4 + ((x + dx) & 3)
                    for h in range(2):
                        source = chip * 2 + (core ^ h)
                        cols = pl.ds(pl.multiple_of(source * 128, 128), 128)
                        part = ref[start : start + step, cols].astype(f32) * factor * gain[:, cols]
                        place_in = a * 256 + h * 128
                        outs[b][rows, place_in : place_in + 128] = part.astype(bf16)


def multiply(rows, parts, cols):
    weights = jnp.concatenate([p[:, cols] for p in parts], axis=0)
    return jnp.dot(rows[...], weights, preferred_element_type=f32)


COLUMNS = [slice(n, n + 256) for n in range(0, 768, 256)]


def project_kernel(own, before, after, *refs):
    out = refs[-1]
    for cols in COLUMNS:
        total = multiply(own, refs[:2], cols) + multiply(before, refs[2:4], cols)
        out[:, cols] = total + multiply(after, refs[4:6], cols)


def query_kernel(place, lengths, across, total, near, far, proj, packed):
    for cols in COLUMNS:
        proj[:, cols] = (total[:, cols] + multiply(across, (near, far), cols)).astype(bf16)
    position, origin = place[3], place[4]
    q = jnp.concatenate(
        [proj[4 * BLK :, HEAD_SIZE * g : HEAD_SIZE * (g + 1)] for g in range(GROUP_HEADS)], axis=0
    )
    sets = []
    for j in range(5):
        keys = BLK if j < 4 else QTOK
        here = slice(j * BLK, j * BLK + keys)
        scores = lax.dot_general(
            q, proj[here, 512:640], (((1,), (1,)), ((), ())), preferred_element_type=f32
        ) * SCALE
        col = lax.broadcasted_iota(jnp.int32, (PAIRS, keys), 1)
        if j < 4:
            allowed = col < lengths[position ^ ((j & 1) | ((j >> 1) << 5))]
        else:
            allowed = col <= (lax.broadcasted_iota(jnp.int32, (PAIRS, keys), 0) & (QTOK - 1))
        scores = jnp.where(allowed, scores, -jnp.inf)
        peak = jnp.max(scores, axis=-1, keepdims=True)
        weights = jnp.exp(scores - peak)
        sum_exp = jnp.sum(weights, axis=-1, keepdims=True)
        numerator = jnp.dot(weights.astype(bf16), proj[here, 640:768], preferred_element_type=f32)
        if j == 4:
            peak = jnp.where(origin == 1, peak, -jnp.inf)
        sets.append((peak, sum_exp, numerator))
    peak = functools.reduce(jnp.maximum, [s[0] for s in sets])
    scales = [jnp.exp(s[0] - peak) for s in sets]
    total_exp = sum(s[1] * w for s, w in zip(sets, scales))
    numerator = sum(s[2] * w for s, w in zip(sets, scales))
    lane = lax.broadcasted_iota(jnp.int32, (PAIRS, HEAD_SIZE), 1)
    stats = jnp.where(lane < 64, peak, total_exp)
    start = pl.multiple_of(place[5] * BLK, BLK)
    anchor_rows = proj[pl.ds(start, BLK), 512:768].astype(f32)
    for t in range(CHIPS):
        packed[t, :SHARE, :HEAD_SIZE] = numerator[t * SHARE : (t + 1) * SHARE]
        packed[t, :SHARE, HEAD_SIZE:] = stats[t * SHARE : (t + 1) * SHARE]
        packed[t, SHARE:, :] = anchor_rows[t * ANCHOR_SHARE : (t + 1) * ANCHOR_SHARE]


def merge(parts):
    peaks = [s[:, :1] for _, s in parts]
    top = functools.reduce(jnp.maximum, peaks)
    scales = [jnp.exp(p - top) for p in peaks]
    total = sum(s[:, 127:] * w for (_, s), w in zip(parts, scales))
    numerator = sum(n * w for (n, _), w in zip(parts, scales))
    return top, total, numerator


def merge_plane_kernel(parts, out):
    top, total, numerator = merge(
        [(parts[t, :SHARE, :HEAD_SIZE], parts[t, :SHARE, HEAD_SIZE:]) for t in range(CHIPS)]
    )
    lane = lax.broadcasted_iota(jnp.int32, (SHARE, HEAD_SIZE), 1)
    out[:SHARE, :HEAD_SIZE] = numerator
    out[:SHARE, HEAD_SIZE:] = jnp.where(lane < 64, top, total)
    out[SHARE:, :] = parts[0, SHARE:, :]


def merge_deep_kernel(place, own, before, after, across, out):
    refs = (own, before, after, across)
    _, total, numerator = merge([(r[:SHARE, :HEAD_SIZE], r[:SHARE, HEAD_SIZE:]) for r in refs])
    out[:SHARE, :] = numerator / total
    zg = place[6]
    anchor = own[SHARE:, :]
    for source, ref in ((1, before), (3, after), (2, across)):
        anchor = jnp.where(zg == source, ref[SHARE:, :], anchor)
    out[SHARE : SHARE + ANCHOR_SHARE, :] = anchor[:, :HEAD_SIZE]
    out[SHARE + ANCHOR_SHARE :, :] = anchor[:, HEAD_SIZE:]


def block_kernel(place, lengths, proj, shared, *outs):
    position = place[3]
    anchor_k = shared[:, SHARE : SHARE + ANCHOR_SHARE, :].reshape(BLK, HEAD_SIZE).astype(bf16)
    anchor_v = shared[:, SHARE + ANCHOR_SHARE :, :].reshape(BLK, HEAD_SIZE).astype(bf16)
    query_out = shared[:, :SHARE, :].reshape(PAIRS, HEAD_SIZE).astype(bf16)
    rows = GROUP_HEADS * BLK
    col = lax.broadcasted_iota(jnp.int32, (rows, 2 * BLK), 1)
    row = lax.broadcasted_iota(jnp.int32, (rows, 2 * BLK), 0) & (BLK - 1)
    for j in range(4):
        block = position ^ ((j & 1) | ((j >> 1) << 5))
        anchor_length = jnp.where(block > 0, lengths[0], 0)
        allowed = (col < anchor_length) | (
            (col >= BLK) & (col - BLK <= row) & (col - BLK < lengths[block])
        )
        here = slice(j * BLK, (j + 1) * BLK)
        q = jnp.concatenate(
            [proj[here, HEAD_SIZE * g : HEAD_SIZE * (g + 1)] for g in range(GROUP_HEADS)], axis=0
        )
        k = jnp.concatenate([anchor_k, proj[here, 512:640]], axis=0)
        v = jnp.concatenate([anchor_v, proj[here, 640:768]], axis=0)
        scores = lax.dot_general(q, k, (((1,), (1,)), ((), ())), preferred_element_type=f32) * SCALE
        scores = jnp.where(allowed, scores, -jnp.inf)
        peak = jnp.max(scores, axis=-1, keepdims=True)
        weights = jnp.exp(scores - peak)
        total = jnp.sum(weights, axis=-1, keepdims=True)
        numerator = jnp.dot(weights.astype(bf16), v, preferred_element_type=f32)
        result = (numerator / total).astype(bf16)
        for g in range(GROUP_HEADS):
            cols = slice(HEAD_SIZE * g, HEAD_SIZE * (g + 1))
            outs[j][:BLK, cols] = result[g * BLK : (g + 1) * BLK]
            outs[j][BLK:, cols] = query_out[g * QTOK : (g + 1) * QTOK]


def assemble_kernel(place, *refs):
    parts, block_out, query_out = refs[:4], refs[4], refs[5]
    for j in range(4):
        cols = pl.ds(pl.multiple_of((place[5] ^ j) * 512, 512), 512)
        block_out[:, cols] = parts[j][:BLK, :]
        query_out[:, cols] = parts[j][BLK:, :]


def shapes(*items):
    return tuple(jax.ShapeDtypeStruct(s, d) for s, d in items)


def call(kernel, out_shape, n_smem, n_vmem, flops=0, size=0):
    return pl.pallas_call(
        kernel,
        out_shape=out_shape,
        in_specs=[SMEM] * n_smem + [VMEM] * n_vmem,
        out_specs=jax.tree.map(lambda _: VMEM, out_shape),
        compiler_params=pltpu.CompilerParams(vmem_limit_bytes=40 << 20),
        cost_estimate=pl.CostEstimate(flops=flops, bytes_accessed=size, transcendentals=0),
    )


def per_device(context, query_acts, norm_gain, w_query, w_key, value_weight, lengths):
    zg, zi, y, x, core = (lax.axis_index(a).astype(jnp.int32) for a in AXES)
    head = zi * 2 + core
    position = ((zg * 2 + zi) * 16 + y * 4 + x) * 2 + core
    origin = ((zg == 0) & (y == 0) & (x == 0)).astype(jnp.int32)
    place = jnp.stack([y, x, core, position, origin, head, zg, zi])

    def columns(h):
        cut = lambda w, width: lax.dynamic_slice(w, (0, h * width), (w.shape[0], width))
        return jnp.concatenate([cut(w_query, 512), cut(w_key, 128), cut(value_weight, 128)], axis=1)

    theirs = columns(zi * 2 + 1 - core)
    w_own, w_before, w_after, w_across = gather_weights(columns(head), theirs)

    z_mate = lax.ppermute(context, "zi", SWAP)
    core_mate = lax.ppermute(context, "core", SWAP)
    z_mate, _ = lax.optimization_barrier((z_mate, w_own[1]))
    zc_mate = lax.ppermute(z_mate, "core", SWAP)
    rows = 4 * BLK + QTOK
    x_own, x_before, x_after, x_across = call(
        prepare_kernel, shapes(*[((rows, 1024), bf16)] * 4), 1, 6, 1 << 24, 10 << 20
    )(place, context, core_mate, z_mate, zc_mate, query_acts, norm_gain[None])

    total = call(
        project_kernel, jax.ShapeDtypeStruct((rows, 768), f32), 0, 9, 27 << 27, 12 << 20
    )(x_own, x_before, x_after, *w_own, *w_before, *w_after)
    proj, packed = call(
        query_kernel,
        shapes(((rows, 768), bf16), ((CHIPS, SHARE + ANCHOR_SHARE, 256), f32)), 2, 4, 9 << 27, 6 << 20,
    )(place, lengths, x_across, total, *w_across)
    gathered = lax.all_to_all(packed, PLANE, 0, 0, tiled=True)
    merged = call(
        merge_plane_kernel, jax.ShapeDtypeStruct((SHARE + ANCHOR_SHARE, 256), f32), 0, 1, 1 << 20, 1 << 19
    )(gathered)
    deep = lambda k: lax.ppermute(merged, "zg", [(i, (i + k) % 4) for i in range(4)])
    final = call(
        merge_deep_kernel,
        jax.ShapeDtypeStruct((SHARE + 2 * ANCHOR_SHARE, HEAD_SIZE), f32), 1, 4, 1 << 20, 1 << 17,
    )(place, merged, deep(1), deep(-1), deep(2)).astype(bf16)
    shared = lax.all_to_all(
        jnp.broadcast_to(final[None], (CHIPS, *final.shape)), PLANE, 0, 0, tiled=True
    )
    pieces = call(
        block_kernel, shapes(*[((BLK + QTOK, 512), bf16)] * 4), 2, 2, 1 << 29, 3 << 20
    )(place, lengths, proj, shared)
    from_z = lax.ppermute(pieces[2], "zi", SWAP)
    from_zc = lax.ppermute(pieces[3], ("zi", "core"), [(i, 3 - i) for i in range(4)])
    to_core, from_z = lax.optimization_barrier((pieces[1], from_z))
    received = (pieces[0], lax.ppermute(to_core, "core", SWAP), from_z, from_zc)
    return call(
        assemble_kernel, shapes(((BLK, 2048), bf16), ((QTOK, 2048), bf16)), 1, 4, 0, 2 << 20
    )(place, *received)


def solution(mesh):
    grid = Mesh(mesh.devices.reshape(4, 2, 4, 4, 2), AXES)
    own_rows, width = P(AXES, None), P(YXC, None)
    return jax.shard_map(
        per_device,
        mesh=grid,
        in_specs=(own_rows, P(), P(), width, width, width, P()),
        out_specs=(own_rows, P()),
        check_vma=False,
    )
```

```python
import functools

import jax
import jax.numpy as jnp
from jax import lax
from jax.experimental import pallas as pl
from jax.experimental.pallas import tpu as pltpu
from jax.sharding import Mesh
from jax.sharding import PartitionSpec as P

HEAD_SIZE = 128
GROUP_HEADS = 4
BLK = 128
QTOK = 64
PAIRS = GROUP_HEADS * QTOK
CHIPS = 16
SHARE = PAIRS // CHIPS
ANCHOR_SHARE = BLK // CHIPS
SCALE = HEAD_SIZE ** (-0.5)
EPSILON = 1e-05
AXES = ("zg", "zi", "y", "x", "core")
PLANE = ("y", "x")
YXC = ("y", "x", "core")
OFFSETS = (0, -1, 1, 2)
bf16 = jnp.bfloat16
f32 = jnp.float32
VMEM = pl.BlockSpec(memory_space=pltpu.VMEM)
SMEM = pl.BlockSpec(memory_space=pltpu.SMEM)
SWAP = [(0, 1), (1, 0)]


def device_index(y, x, core):
    return (y * 4 + x) * 2 + core


def torus_pairs(step, first):
    pairs = []
    for y in range(4):
        for x in range(4):
            for core in range(2):
                along_x = (core == 0) == first
                to = (y, (x + step) % 4) if along_x else ((y + step) % 4, x)
                pairs.append((device_index(y, x, core), device_index(*to, core)))
    return pairs


def send(rows, step, first):
    return lax.ppermute(rows, YXC, torus_pairs(step, first))


def join(top, bottom):
    return jnp.concatenate([top, bottom], axis=0)


def join_kernel(top, bottom, out):
    out[:256, :] = top[...]
    out[256:, :] = bottom[...]


def gather_weights(mine, theirs):
    mate = lax.ppermute(theirs, "core", SWAP)
    own = join(mine, mate)
    before, after = send(own, 1, True), send(own, -1, True)
    across = send(own, 2, True)
    pair = lambda top, bottom: call(
        join_kernel, jax.ShapeDtypeStruct((512, 768), bf16), 0, 2, 0, 3 << 19
    )(top, bottom)
    near, far = pair(own, before), pair(after, across)
    near_before, far_after = send(near, 1, False), send(far, -1, False)
    far_before, near_after = send(far, 1, False), send(near, -1, False)
    near_across, far_across = send(near_before, 1, False), send(far_after, -1, False)
    return (near, far), (near_before, far_before), (near_after, far_after), (near_across, far_across)


def prepare_kernel(place, own, core_mate, z_mate, zc_mate, query, gain, *outs):
    y, x, core = place[0], place[1], place[2]
    step = 64
    for number, ref in enumerate((own, core_mate, z_mate, zc_mate, query)):
        for start in range(0, ref.shape[0], step):
            widened = ref[start : start + step, :].astype(f32)
            factor = lax.rsqrt(jnp.mean(widened * widened, axis=-1, keepdims=True) + EPSILON)
            rows = slice(number * BLK + start, number * BLK + start + step)
            for b in range(4):
                for a in range(4):
                    dx = jnp.where(core == 0, OFFSETS[a], OFFSETS[b])
                    dy = jnp.where(core == 0, OFFSETS[b], OFFSETS[a])
                    chip = ((y + dy) & 3) * 4 + ((x + dx) & 3)
                    for h in range(2):
                        source = chip * 2 + (core ^ h)
                        cols = pl.ds(pl.multiple_of(source * 128, 128), 128)
                        part = ref[start : start + step, cols].astype(f32) * factor * gain[:, cols]
                        place_in = a * 256 + h * 128
                        outs[b][rows, place_in : place_in + 128] = part.astype(bf16)


def multiply(rows, parts, cols):
    weights = jnp.concatenate([p[:, cols] for p in parts], axis=0)
    return jnp.dot(rows[...], weights, preferred_element_type=f32)


COLUMNS = [slice(n, n + 256) for n in range(0, 768, 256)]


def project_kernel(own, before, after, *refs):
    out = refs[-1]
    for cols in COLUMNS:
        total = multiply(own, refs[:2], cols) + multiply(before, refs[2:4], cols)
        out[:, cols] = total + multiply(after, refs[4:6], cols)


def query_kernel(place, lengths, across, total, near, far, proj, packed):
    for cols in COLUMNS:
        proj[:, cols] = (total[:, cols] + multiply(across, (near, far), cols)).astype(bf16)
    position, origin = place[3], place[4]
    q = jnp.concatenate(
        [proj[4 * BLK :, HEAD_SIZE * g : HEAD_SIZE * (g + 1)] for g in range(GROUP_HEADS)], axis=0
    )
    sets = []
    for j in range(5):
        keys = BLK if j < 4 else QTOK
        here = slice(j * BLK, j * BLK + keys)
        scores = lax.dot_general(
            q, proj[here, 512:640], (((1,), (1,)), ((), ())), preferred_element_type=f32
        ) * SCALE
        col = lax.broadcasted_iota(jnp.int32, (PAIRS, keys), 1)
        if j < 4:
            allowed = col < lengths[position ^ ((j & 1) | ((j >> 1) << 5))]
        else:
            allowed = col <= (lax.broadcasted_iota(jnp.int32, (PAIRS, keys), 0) & (QTOK - 1))
        scores = jnp.where(allowed, scores, -jnp.inf)
        peak = jnp.max(scores, axis=-1, keepdims=True)
        weights = jnp.exp(scores - peak)
        sum_exp = jnp.sum(weights, axis=-1, keepdims=True)
        numerator = jnp.dot(weights.astype(bf16), proj[here, 640:768], preferred_element_type=f32)
        if j == 4:
            peak = jnp.where(origin == 1, peak, -jnp.inf)
        sets.append((peak, sum_exp, numerator))
    peak = functools.reduce(jnp.maximum, [s[0] for s in sets])
    scales = [jnp.exp(s[0] - peak) for s in sets]
    total_exp = sum(s[1] * w for s, w in zip(sets, scales))
    numerator = sum(s[2] * w for s, w in zip(sets, scales))
    lane = lax.broadcasted_iota(jnp.int32, (PAIRS, HEAD_SIZE), 1)
    stats = jnp.where(lane < 64, peak, total_exp)
    start = pl.multiple_of(place[5] * BLK, BLK)
    anchor_rows = proj[pl.ds(start, BLK), 512:768].astype(f32)
    for t in range(CHIPS):
        packed[t, :SHARE, :HEAD_SIZE] = numerator[t * SHARE : (t + 1) * SHARE]
        packed[t, :SHARE, HEAD_SIZE:] = stats[t * SHARE : (t + 1) * SHARE]
        packed[t, SHARE:, :] = anchor_rows[t * ANCHOR_SHARE : (t + 1) * ANCHOR_SHARE]


def merge(parts):
    peaks = [s[:, :1] for _, s in parts]
    top = functools.reduce(jnp.maximum, peaks)
    scales = [jnp.exp(p - top) for p in peaks]
    total = sum(s[:, 127:] * w for (_, s), w in zip(parts, scales))
    numerator = sum(n * w for (n, _), w in zip(parts, scales))
    return top, total, numerator


def merge_plane_kernel(parts, out):
    top, total, numerator = merge(
        [(parts[t, :SHARE, :HEAD_SIZE], parts[t, :SHARE, HEAD_SIZE:]) for t in range(CHIPS)]
    )
    lane = lax.broadcasted_iota(jnp.int32, (SHARE, HEAD_SIZE), 1)
    out[:SHARE, :HEAD_SIZE] = numerator
    out[:SHARE, HEAD_SIZE:] = jnp.where(lane < 64, top, total)
    out[SHARE:, :] = parts[0, SHARE:, :]


def merge_deep_kernel(place, own, before, after, across, out):
    refs = (own, before, after, across)
    _, total, numerator = merge([(r[:SHARE, :HEAD_SIZE], r[:SHARE, HEAD_SIZE:]) for r in refs])
    out[:SHARE, :] = numerator / total
    zg = place[6]
    anchor = own[SHARE:, :]
    for source, ref in ((1, before), (3, after), (2, across)):
        anchor = jnp.where(zg == source, ref[SHARE:, :], anchor)
    out[SHARE : SHARE + ANCHOR_SHARE, :] = anchor[:, :HEAD_SIZE]
    out[SHARE + ANCHOR_SHARE :, :] = anchor[:, HEAD_SIZE:]


def block_kernel(place, lengths, proj, shared, *outs):
    position = place[3]
    anchor_k = shared[:, SHARE : SHARE + ANCHOR_SHARE, :].reshape(BLK, HEAD_SIZE).astype(bf16)
    anchor_v = shared[:, SHARE + ANCHOR_SHARE :, :].reshape(BLK, HEAD_SIZE).astype(bf16)
    query_out = shared[:, :SHARE, :].reshape(PAIRS, HEAD_SIZE).astype(bf16)
    rows = GROUP_HEADS * BLK
    col = lax.broadcasted_iota(jnp.int32, (rows, 2 * BLK), 1)
    row = lax.broadcasted_iota(jnp.int32, (rows, 2 * BLK), 0) & (BLK - 1)
    for j in range(4):
        block = position ^ ((j & 1) | ((j >> 1) << 5))
        anchor_length = jnp.where(block > 0, lengths[0], 0)
        allowed = (col < anchor_length) | (
            (col >= BLK) & (col - BLK <= row) & (col - BLK < lengths[block])
        )
        here = slice(j * BLK, (j + 1) * BLK)
        q = jnp.concatenate(
            [proj[here, HEAD_SIZE * g : HEAD_SIZE * (g + 1)] for g in range(GROUP_HEADS)], axis=0
        )
        k = jnp.concatenate([anchor_k, proj[here, 512:640]], axis=0)
        v = jnp.concatenate([anchor_v, proj[here, 640:768]], axis=0)
        scores = lax.dot_general(q, k, (((1,), (1,)), ((), ())), preferred_element_type=f32) * SCALE
        scores = jnp.where(allowed, scores, -jnp.inf)
        peak = jnp.max(scores, axis=-1, keepdims=True)
        weights = jnp.exp(scores - peak)
        total = jnp.sum(weights, axis=-1, keepdims=True)
        numerator = jnp.dot(weights.astype(bf16), v, preferred_element_type=f32)
        result = (numerator / total).astype(bf16)
        for g in range(GROUP_HEADS):
            cols = slice(HEAD_SIZE * g, HEAD_SIZE * (g + 1))
            outs[j][:BLK, cols] = result[g * BLK : (g + 1) * BLK]
            outs[j][BLK:, cols] = query_out[g * QTOK : (g + 1) * QTOK]


def assemble_kernel(place, *refs):
    parts, block_out, query_out = refs[:4], refs[4], refs[5]
    for j in range(4):
        cols = pl.ds(pl.multiple_of((place[5] ^ j) * 512, 512), 512)
        block_out[:, cols] = parts[j][:BLK, :]
        query_out[:, cols] = parts[j][BLK:, :]


def shapes(*items):
    return tuple(jax.ShapeDtypeStruct(s, d) for s, d in items)


def call(kernel, out_shape, n_smem, n_vmem, flops=0, size=0):
    return pl.pallas_call(
        kernel,
        out_shape=out_shape,
        in_specs=[SMEM] * n_smem + [VMEM] * n_vmem,
        out_specs=jax.tree.map(lambda _: VMEM, out_shape),
        compiler_params=pltpu.CompilerParams(vmem_limit_bytes=40 << 20),
        cost_estimate=pl.CostEstimate(flops=flops, bytes_accessed=size, transcendentals=0),
    )


def per_device(context, query_acts, norm_gain, w_query, w_key, value_weight, lengths):
    zg, zi, y, x, core = (lax.axis_index(a).astype(jnp.int32) for a in AXES)
    head = zi * 2 + core
    position = ((zg * 2 + zi) * 16 + y * 4 + x) * 2 + core
    origin = ((zg == 0) & (y == 0) & (x == 0)).astype(jnp.int32)
    place = jnp.stack([y, x, core, position, origin, head, zg, zi])

    def columns(h):
        cut = lambda w, width: lax.dynamic_slice(w, (0, h * width), (w.shape[0], width))
        return jnp.concatenate([cut(w_query, 512), cut(w_key, 128), cut(value_weight, 128)], axis=1)

    theirs = columns(zi * 2 + 1 - core)
    w_own, w_before, w_after, w_across = gather_weights(columns(head), theirs)

    z_mate = lax.ppermute(context, "zi", SWAP)
    core_mate = lax.ppermute(context, "core", SWAP)
    z_mate, _ = lax.optimization_barrier((z_mate, w_own[0]))
    zc_mate = lax.ppermute(z_mate, "core", SWAP)
    rows = 4 * BLK + QTOK
    x_own, x_before, x_after, x_across = call(
        prepare_kernel, shapes(*[((rows, 1024), bf16)] * 4), 1, 6, 1 << 24, 10 << 20
    )(place, context, core_mate, z_mate, zc_mate, query_acts, norm_gain[None])

    total = call(
        project_kernel, jax.ShapeDtypeStruct((rows, 768), f32), 0, 9, 27 << 27, 12 << 20
    )(x_own, x_before, x_after, *w_own, *w_before, *w_after)
    proj, packed = call(
        query_kernel,
        shapes(((rows, 768), bf16), ((CHIPS, SHARE + ANCHOR_SHARE, 256), f32)), 2, 4, 9 << 27, 6 << 20,
    )(place, lengths, x_across, total, *w_across)
    gathered = lax.all_to_all(packed, PLANE, 0, 0, tiled=True)
    merged = call(
        merge_plane_kernel, jax.ShapeDtypeStruct((SHARE + ANCHOR_SHARE, 256), f32), 0, 1, 1 << 20, 1 << 19
    )(gathered)
    deep = lambda k: lax.ppermute(merged, "zg", [(i, (i + k) % 4) for i in range(4)])
    final = call(
        merge_deep_kernel,
        jax.ShapeDtypeStruct((SHARE + 2 * ANCHOR_SHARE, HEAD_SIZE), f32), 1, 4, 1 << 20, 1 << 17,
    )(place, merged, deep(1), deep(-1), deep(2)).astype(bf16)
    shared = lax.all_to_all(
        jnp.broadcast_to(final[None], (CHIPS, *final.shape)), PLANE, 0, 0, tiled=True
    )
    pieces = call(
        block_kernel, shapes(*[((BLK + QTOK, 512), bf16)] * 4), 2, 2, 1 << 29, 3 << 20
    )(place, lengths, proj, shared)
    from_z = lax.ppermute(pieces[2], "zi", SWAP)
    from_zc = lax.ppermute(pieces[3], ("zi", "core"), [(i, 3 - i) for i in range(4)])
    to_core, from_z = lax.optimization_barrier((pieces[1], from_z))
    received = (pieces[0], lax.ppermute(to_core, "core", SWAP), from_z, from_zc)
    return call(
        assemble_kernel, shapes(((BLK, 2048), bf16), ((QTOK, 2048), bf16)), 1, 4, 0, 2 << 20
    )(place, *received)


def solution(mesh):
    grid = Mesh(mesh.devices.reshape(4, 2, 4, 4, 2), AXES)
    own_rows, width = P(AXES, None), P(YXC, None)
    return jax.shard_map(
        per_device,
        mesh=grid,
        in_specs=(own_rows, P(), P(), width, width, width, P()),
        out_specs=(own_rows, P()),
        check_vma=False,
    )
```

```python
import functools

import jax
import jax.numpy as jnp
from jax import lax
from jax.experimental import pallas as pl
from jax.experimental.pallas import tpu as pltpu
from jax.sharding import Mesh
from jax.sharding import PartitionSpec as P

HEAD_SIZE = 128
GROUP_HEADS = 4
BLK = 128
QTOK = 64
PAIRS = GROUP_HEADS * QTOK
CHIPS = 16
SHARE = PAIRS // CHIPS
ANCHOR_SHARE = BLK // CHIPS
SCALE = HEAD_SIZE ** (-0.5)
EPSILON = 1e-05
AXES = ("zg", "zi", "y", "x", "core")
PLANE = ("y", "x")
YXC = ("y", "x", "core")
OFFSETS = (0, -1, 1, 2)
bf16 = jnp.bfloat16
f32 = jnp.float32
VMEM = pl.BlockSpec(memory_space=pltpu.VMEM)
SMEM = pl.BlockSpec(memory_space=pltpu.SMEM)
SWAP = [(0, 1), (1, 0)]


def device_index(y, x, core):
    return (y * 4 + x) * 2 + core


def torus_pairs(step, first):
    pairs = []
    for y in range(4):
        for x in range(4):
            for core in range(2):
                along_x = (core == 0) == first
                to = (y, (x + step) % 4) if along_x else ((y + step) % 4, x)
                pairs.append((device_index(y, x, core), device_index(*to, core)))
    return pairs


def send(rows, step, first):
    return lax.ppermute(rows, YXC, torus_pairs(step, first))


def join(top, bottom):
    return jnp.concatenate([top, bottom], axis=0)


def join_kernel(top, bottom, out):
    out[:256, :] = top[...]
    out[256:, :] = bottom[...]


def gather_weights(mine, theirs):
    mate = lax.ppermute(theirs, "core", SWAP)
    own = join(mine, mate)
    before, after = send(own, 1, True), send(own, -1, True)
    across = send(own, 2, True)
    pair = lambda top, bottom: call(
        join_kernel, jax.ShapeDtypeStruct((512, 768), bf16), 0, 2, 0, 3 << 19
    )(top, bottom)
    near, far = pair(own, before), pair(after, across)
    near_before, far_after = send(near, 1, False), send(far, -1, False)
    far_before, near_after = send(far, 1, False), send(near, -1, False)
    near_across, far_across = send(near_before, 1, False), send(far_after, -1, False)
    return (near, far), (near_before, far_before), (near_after, far_after), (near_across, far_across)


def prepare_kernel(place, own, core_mate, z_mate, zc_mate, query, gain, *outs):
    y, x, core = place[0], place[1], place[2]
    step = 64
    for number, ref in enumerate((own, core_mate, z_mate, zc_mate, query)):
        for start in range(0, ref.shape[0], step):
            widened = ref[start : start + step, :].astype(f32)
            factor = lax.rsqrt(jnp.mean(widened * widened, axis=-1, keepdims=True) + EPSILON)
            rows = slice(number * BLK + start, number * BLK + start + step)
            for b in range(4):
                for a in range(4):
                    dx = jnp.where(core == 0, OFFSETS[a], OFFSETS[b])
                    dy = jnp.where(core == 0, OFFSETS[b], OFFSETS[a])
                    chip = ((y + dy) & 3) * 4 + ((x + dx) & 3)
                    for h in range(2):
                        source = chip * 2 + (core ^ h)
                        cols = pl.ds(pl.multiple_of(source * 128, 128), 128)
                        part = ref[start : start + step, cols].astype(f32) * factor * gain[:, cols]
                        place_in = a * 256 + h * 128
                        outs[b][rows, place_in : place_in + 128] = part.astype(bf16)


def multiply(rows, parts, cols):
    weights = jnp.concatenate([p[:, cols] for p in parts], axis=0)
    return jnp.dot(rows[...], weights, preferred_element_type=f32)


COLUMNS = [slice(n, n + 256) for n in range(0, 768, 256)]


def project_kernel(own, before, after, *refs):
    out = refs[-1]
    for cols in COLUMNS:
        total = multiply(own, refs[:2], cols) + multiply(before, refs[2:4], cols)
        out[:, cols] = total + multiply(after, refs[4:6], cols)


def query_kernel(place, lengths, across, total, near, far, proj, packed):
    for cols in COLUMNS:
        proj[:, cols] = (total[:, cols] + multiply(across, (near, far), cols)).astype(bf16)
    position, origin = place[3], place[4]
    q = jnp.concatenate(
        [proj[4 * BLK :, HEAD_SIZE * g : HEAD_SIZE * (g + 1)] for g in range(GROUP_HEADS)], axis=0
    )
    sets = []
    for j in range(5):
        keys = BLK if j < 4 else QTOK
        here = slice(j * BLK, j * BLK + keys)
        scores = lax.dot_general(
            q, proj[here, 512:640], (((1,), (1,)), ((), ())), preferred_element_type=f32
        ) * SCALE
        col = lax.broadcasted_iota(jnp.int32, (PAIRS, keys), 1)
        if j < 4:
            allowed = col < lengths[position ^ ((j & 1) | ((j >> 1) << 5))]
        else:
            allowed = col <= (lax.broadcasted_iota(jnp.int32, (PAIRS, keys), 0) & (QTOK - 1))
        scores = jnp.where(allowed, scores, -jnp.inf)
        peak = jnp.max(scores, axis=-1, keepdims=True)
        weights = jnp.exp(scores - peak)
        sum_exp = jnp.sum(weights, axis=-1, keepdims=True)
        numerator = jnp.dot(weights.astype(bf16), proj[here, 640:768], preferred_element_type=f32)
        if j == 4:
            peak = jnp.where(origin == 1, peak, -jnp.inf)
        sets.append((peak, sum_exp, numerator))
    peak = functools.reduce(jnp.maximum, [s[0] for s in sets])
    scales = [jnp.exp(s[0] - peak) for s in sets]
    total_exp = sum(s[1] * w for s, w in zip(sets, scales))
    numerator = sum(s[2] * w for s, w in zip(sets, scales))
    lane = lax.broadcasted_iota(jnp.int32, (PAIRS, HEAD_SIZE), 1)
    stats = jnp.where(lane < 64, peak, total_exp)
    start = pl.multiple_of(place[5] * BLK, BLK)
    anchor_rows = proj[pl.ds(start, BLK), 512:768].astype(f32)
    for t in range(CHIPS):
        packed[t, :SHARE, :HEAD_SIZE] = numerator[t * SHARE : (t + 1) * SHARE]
        packed[t, :SHARE, HEAD_SIZE:] = stats[t * SHARE : (t + 1) * SHARE]
        packed[t, SHARE:, :] = anchor_rows[t * ANCHOR_SHARE : (t + 1) * ANCHOR_SHARE]


def merge(parts):
    peaks = [s[:, :1] for _, s in parts]
    top = functools.reduce(jnp.maximum, peaks)
    scales = [jnp.exp(p - top) for p in peaks]
    total = sum(s[:, 127:] * w for (_, s), w in zip(parts, scales))
    numerator = sum(n * w for (n, _), w in zip(parts, scales))
    return top, total, numerator


def merge_plane_kernel(parts, out):
    top, total, numerator = merge(
        [(parts[t, :SHARE, :HEAD_SIZE], parts[t, :SHARE, HEAD_SIZE:]) for t in range(CHIPS)]
    )
    lane = lax.broadcasted_iota(jnp.int32, (SHARE, HEAD_SIZE), 1)
    out[:SHARE, :HEAD_SIZE] = numerator
    out[:SHARE, HEAD_SIZE:] = jnp.where(lane < 64, top, total)
    out[SHARE:, :] = parts[0, SHARE:, :]


def merge_deep_kernel(place, own, before, after, across, out):
    refs = (own, before, after, across)
    _, total, numerator = merge([(r[:SHARE, :HEAD_SIZE], r[:SHARE, HEAD_SIZE:]) for r in refs])
    zg = place[6]
    anchor = own[SHARE:, :]
    for source, ref in ((1, before), (3, after), (2, across)):
        anchor = jnp.where(zg == source, ref[SHARE:, :], anchor)
    parts = [numerator / total, anchor[:, :HEAD_SIZE], anchor[:, HEAD_SIZE:]]
    out[...] = jnp.concatenate(parts, axis=0).astype(bf16)


def block_kernel(place, lengths, proj, shared, *outs):
    position = place[3]
    anchor_k = shared[:, SHARE : SHARE + ANCHOR_SHARE, :].reshape(BLK, HEAD_SIZE).astype(bf16)
    anchor_v = shared[:, SHARE + ANCHOR_SHARE :, :].reshape(BLK, HEAD_SIZE).astype(bf16)
    query_out = shared[:, :SHARE, :].reshape(PAIRS, HEAD_SIZE).astype(bf16)
    rows = GROUP_HEADS * BLK
    col = lax.broadcasted_iota(jnp.int32, (rows, 2 * BLK), 1)
    row = lax.broadcasted_iota(jnp.int32, (rows, 2 * BLK), 0) & (BLK - 1)
    for j in range(4):
        block = position ^ ((j & 1) | ((j >> 1) << 5))
        anchor_length = jnp.where(block > 0, lengths[0], 0)
        allowed = (col < anchor_length) | (
            (col >= BLK) & (col - BLK <= row) & (col - BLK < lengths[block])
        )
        here = slice(j * BLK, (j + 1) * BLK)
        q = jnp.concatenate(
            [proj[here, HEAD_SIZE * g : HEAD_SIZE * (g + 1)] for g in range(GROUP_HEADS)], axis=0
        )
        k = jnp.concatenate([anchor_k, proj[here, 512:640]], axis=0)
        v = jnp.concatenate([anchor_v, proj[here, 640:768]], axis=0)
        scores = lax.dot_general(q, k, (((1,), (1,)), ((), ())), preferred_element_type=f32) * SCALE
        scores = jnp.where(allowed, scores, -jnp.inf)
        peak = jnp.max(scores, axis=-1, keepdims=True)
        weights = jnp.exp(scores - peak)
        total = jnp.sum(weights, axis=-1, keepdims=True)
        numerator = jnp.dot(weights.astype(bf16), v, preferred_element_type=f32)
        result = (numerator / total).astype(bf16)
        for g in range(GROUP_HEADS):
            cols = slice(HEAD_SIZE * g, HEAD_SIZE * (g + 1))
            outs[j][:BLK, cols] = result[g * BLK : (g + 1) * BLK]
            outs[j][BLK:, cols] = query_out[g * QTOK : (g + 1) * QTOK]


def assemble_kernel(place, *refs):
    parts, block_out, query_out = refs[:4], refs[4], refs[5]
    for j in range(4):
        cols = pl.ds(pl.multiple_of((place[5] ^ j) * 512, 512), 512)
        block_out[:, cols] = parts[j][:BLK, :]
        query_out[:, cols] = parts[j][BLK:, :]


def shapes(*items):
    return tuple(jax.ShapeDtypeStruct(s, d) for s, d in items)


def call(kernel, out_shape, n_smem, n_vmem, flops=0, size=0):
    return pl.pallas_call(
        kernel,
        out_shape=out_shape,
        in_specs=[SMEM] * n_smem + [VMEM] * n_vmem,
        out_specs=jax.tree.map(lambda _: VMEM, out_shape),
        compiler_params=pltpu.CompilerParams(vmem_limit_bytes=40 << 20),
        cost_estimate=pl.CostEstimate(flops=flops, bytes_accessed=size, transcendentals=0),
    )


def per_device(context, query_acts, norm_gain, w_query, w_key, value_weight, lengths):
    zg, zi, y, x, core = (lax.axis_index(a).astype(jnp.int32) for a in AXES)
    head = zi * 2 + core
    position = ((zg * 2 + zi) * 16 + y * 4 + x) * 2 + core
    origin = ((zg == 0) & (y == 0) & (x == 0)).astype(jnp.int32)
    place = jnp.stack([y, x, core, position, origin, head, zg, zi])

    def columns(h):
        cut = lambda w, width: lax.dynamic_slice(w, (0, h * width), (w.shape[0], width))
        return jnp.concatenate([cut(w_query, 512), cut(w_key, 128), cut(value_weight, 128)], axis=1)

    theirs = columns(zi * 2 + 1 - core)
    w_own, w_before, w_after, w_across = gather_weights(columns(head), theirs)

    z_mate = lax.ppermute(context, "zi", SWAP)
    core_mate = lax.ppermute(context, "core", SWAP)
    z_mate, _ = lax.optimization_barrier((z_mate, w_own[0]))
    zc_mate = lax.ppermute(z_mate, "core", SWAP)
    rows = 4 * BLK + QTOK
    x_own, x_before, x_after, x_across = call(
        prepare_kernel, shapes(*[((rows, 1024), bf16)] * 4), 1, 6, 1 << 24, 10 << 20
    )(place, context, core_mate, z_mate, zc_mate, query_acts, norm_gain[None])

    total = call(
        project_kernel, jax.ShapeDtypeStruct((rows, 768), f32), 0, 9, 27 << 27, 12 << 20
    )(x_own, x_before, x_after, *w_own, *w_before, *w_after)
    proj, packed = call(
        query_kernel,
        shapes(((rows, 768), bf16), ((CHIPS, SHARE + ANCHOR_SHARE, 256), f32)), 2, 4, 9 << 27, 6 << 20,
    )(place, lengths, x_across, total, *w_across)
    gathered = lax.all_to_all(packed, PLANE, 0, 0, tiled=True)
    merged = call(
        merge_plane_kernel, jax.ShapeDtypeStruct((SHARE + ANCHOR_SHARE, 256), f32), 0, 1, 1 << 20, 1 << 19
    )(gathered)
    deep = lambda k: lax.ppermute(merged, "zg", [(i, (i + k) % 4) for i in range(4)])
    final = call(
        merge_deep_kernel,
        jax.ShapeDtypeStruct((SHARE + 2 * ANCHOR_SHARE, HEAD_SIZE), bf16), 1, 4, 1 << 20, 1 << 17,
    )(place, merged, deep(1), deep(-1), deep(2))
    shared = lax.all_to_all(
        jnp.broadcast_to(final[None], (CHIPS, *final.shape)), PLANE, 0, 0, tiled=True
    )
    pieces = call(
        block_kernel, shapes(*[((BLK + QTOK, 512), bf16)] * 4), 2, 2, 1 << 29, 3 << 20
    )(place, lengths, proj, shared)
    from_z = lax.ppermute(pieces[2], "zi", SWAP)
    from_zc = lax.ppermute(pieces[3], ("zi", "core"), [(i, 3 - i) for i in range(4)])
    to_core, from_z = lax.optimization_barrier((pieces[1], from_z))
    received = (pieces[0], lax.ppermute(to_core, "core", SWAP), from_z, from_zc)
    return call(
        assemble_kernel, shapes(((BLK, 2048), bf16), ((QTOK, 2048), bf16)), 1, 4, 0, 2 << 20
    )(place, *received)


def solution(mesh):
    grid = Mesh(mesh.devices.reshape(4, 2, 4, 4, 2), AXES)
    own_rows, width = P(AXES, None), P(YXC, None)
    return jax.shard_map(
        per_device,
        mesh=grid,
        in_specs=(own_rows, P(), P(), width, width, width, P()),
        out_specs=(own_rows, P()),
        check_vma=False,
    )
```
